768 devices in a mesh: view: 48 (over z_lo, y, core), tok: 16 (over x, z_hi).
Axes of the slice: x: 4, y: 8, z: 12 (z_hi: 4, z_lo: 3; z = z_hi * 3 + z_lo), core: 2. Of those that a mesh axis runs over, the one named last changes fastest.
Arguments:
- queries: bfloat16 [48, 2048, 2048], P('view', 'tok'), may hold values from -6 to 6
- key_states: bfloat16 [48, 2048, 2048], P('view', 'tok'), may hold values from -6 to 6
- value_states: bfloat16 [48, 2048, 2048], P('view', 'tok'), may hold values from -6 to 6
- grad_output: bfloat16 [48, 2048, 2048], P('view', 'tok'), may hold values from -6 to 6
- counts: int32 [48, 16], replicated, may hold values from 8 to 128, as said below
- matching: int32 [1, 48], P(None, 'view'), may hold values from 0 to 47, as said below
Outputs:
- attended: bfloat16 [48, 2048, 2048], P('view', 'tok')
- grad_queries: bfloat16 [48, 2048, 2048], P('view', 'tok')
- grad_keys: bfloat16 [48, 2048, 2048], P('view', 'tok')
- grad_values: bfloat16 [48, 2048, 2048], P('view', 'tok')
The draws below stay inside these ranges and needn't reach their ends.
Inputs may be any that keep to these rules, and one draw needn't show every extreme that they name: The valid tokens of shard t of view v are its first counts[v, t] positions; every view holds exactly 640 valid tokens, and in every view some shard has all 128 positions valid. In every round each view is paired with one of its two neighbours on the cycle of 48 views, the one before or the one after, and pairs are mutual: matching[r, matching[r, v]] = v.
All inputs are finite; a program needn't handle non-finite values.
Results may differ from the reference program's by a relative error of at most 0.0092.
Values may be sent and summed in bfloat16 or wider, within the bound.
No kernel may reach another device: no remote copies, remote signals or barrier semaphores. Data moves between devices by JAX's collectives and lax.ppermute only.
A program may use at most 32 MiB of HBM per device.

```python
import math
import jax
import jax.numpy as jnp
from jax import lax

TOK_DEV = 128
DH = 128
ROUNDS = 1
HEADS = 16
SHARDS = 16
VIEWS = 48
SEQ = 2048
WIDTH = 2048
VIEW_CAP = 640


def draw_pair(key):
    seeded = jax.random.fold_in(key, 4242)
    query_seed, key_seed = jax.random.split(seeded, 2)
    array_shape = (VIEWS, SEQ, WIDTH)
    queries = jnp.clip(jax.random.normal(query_seed, array_shape, jnp.float32), -6.0, 6.0)
    key_states = jnp.clip(jax.random.normal(key_seed, array_shape, jnp.float32), -6.0, 6.0)
    return (queries, key_states)


def draw_queries(key, part):
    return draw_pair(key)[0].astype(jnp.bfloat16)


def draw_key_states(key, part):
    return draw_pair(key)[1].astype(jnp.bfloat16)


def draw_counts(key, part):
    lowest = TOK_DEV // 16
    extra_all = 5 * SEQ // 16 - SHARDS * lowest - (TOK_DEV - lowest)
    pair_count = (SHARDS - 2) // 2
    last_seed, pair_seed, order_seed = jax.random.split(jax.random.fold_in(key, 515), 3)
    last_extra = jax.random.randint(last_seed, (VIEWS,), 0, min(extra_all, TOK_DEV - lowest) + 1)
    remaining = extra_all - last_extra
    pair_base = remaining // pair_count
    pair_rest = remaining % pair_count
    pair_ids = jnp.arange(pair_count)
    pair_sums = pair_base[:, None] + (pair_ids[None, :] < pair_rest[:, None]).astype(jnp.int32)
    first_share = jax.random.randint(pair_seed, (VIEWS, pair_count), 0, pair_sums + 1)
    second_share = pair_sums - first_share
    full_extra = jnp.full((VIEWS, 1), TOK_DEV - lowest, jnp.int32)
    extras = jnp.concatenate([full_extra, last_extra[:, None], first_share, second_share], axis=1)
    ordering = jax.random.randint(order_seed, (VIEWS, SHARDS), 0, 1 << 20) * SHARDS + jnp.arange(SHARDS)[None, :]
    permuted = jnp.argsort(ordering, axis=1, stable=True)
    shuffled = jnp.take_along_axis(extras, permuted, axis=1)
    return (lowest + shuffled).astype(jnp.int32)


def draw_matching(key, part):
    parity = jax.random.randint(jax.random.fold_in(key, 616), (ROUNDS, 1), 0, 2)
    view_ids = jnp.arange(VIEWS)[None, :]
    forward = (view_ids - parity) % 2 == 0
    partner = jnp.where(forward, (view_ids + 1) % VIEWS, (view_ids + VIEWS - 1) % VIEWS)
    return partner.astype(jnp.int32)


def shard_levels(stream_key, shape, shards, least, largest):
    def one(axis_at, blocks):
        draws = jax.random.uniform(jax.random.fold_in(jax.random.fold_in(stream_key, 6), axis_at), (blocks,), jnp.float32, least / len(shards), largest / len(shards))
        return jnp.repeat(jnp.exp(draws), shape[axis_at] // blocks).reshape((-1,) + (1,) * (len(shape) - axis_at - 1))

    level = one(*shards[0])
    for cut in shards[1:]:
        level = level * one(*cut)
    return level


def scatter_about(key, extent, spread, bound, cuts=(), held_as=jnp.bfloat16):
    factor_of = shard_levels(key, extent, cuts, -0.22, 0.18) if cuts else 1.0
    values = jax.random.normal(key, extent, jnp.float32) * spread * factor_of
    return jnp.minimum(jnp.maximum(values, -bound), bound).astype(held_as)


def setup_inputs(seed: int = 0) -> dict:
    arg_keys = jax.random.split(jax.random.key(seed), 7)
    queries = draw_queries(jax.random.fold_in(arg_keys[6], 71), 0)
    key_states = draw_key_states(jax.random.fold_in(arg_keys[6], 71), 0)
    value_states = scatter_about(arg_keys[2], (VIEWS, SEQ, WIDTH), 1.0, 6.0, ((0, 48), (1, 16)))
    grad_output = scatter_about(arg_keys[3], (VIEWS, SEQ, WIDTH), 1.0, 6.0, ((0, 48), (1, 16)))
    counts = draw_counts(jax.random.fold_in(arg_keys[6], 71), 0)
    matching = draw_matching(jax.random.fold_in(arg_keys[6], 71), 0)
    return dict(queries=queries, key_states=key_states, value_states=value_states, grad_output=grad_output, counts=counts, matching=matching)


NEG_FILL = -1e+30

def upcast_single(array):
    return array.astype(jnp.float32)

def rounded(array):
    return upcast_single(lax.optimization_barrier(array.astype(jnp.bfloat16)))

def layout_tables(shard_counts):
    shard_ids = jnp.arange(SHARDS, dtype=jnp.int32)
    starts = (jnp.cumsum(shard_counts) - shard_counts).astype(jnp.int32)
    packed_ids = jnp.arange(VIEW_CAP, dtype=jnp.int32)
    band = lax.optimization_barrier(jnp.sum((starts[None, :] <= packed_ids[:, None]).astype(jnp.int32), axis=1)).astype(jnp.int32) - 1
    band_start = lax.optimization_barrier(jnp.sum(jnp.where(band[:, None] == shard_ids[None, :], starts[None, :], 0), axis=1)).astype(jnp.int32)
    slot_of = (band * TOK_DEV + packed_ids - band_start).astype(jnp.int32)
    slot_ids = jnp.arange(SEQ, dtype=jnp.int32)
    inner = slot_ids % TOK_DEV
    owner = (slot_ids // TOK_DEV)[:, None] == shard_ids[None, :]
    owner_count = lax.optimization_barrier(jnp.sum(jnp.where(owner, shard_counts[None, :], 0), axis=1)).astype(jnp.int32)
    owner_start = lax.optimization_barrier(jnp.sum(jnp.where(owner, starts[None, :], 0), axis=1)).astype(jnp.int32)
    valid = inner < owner_count
    packed_of = jnp.where(valid, owner_start + inner, 0).astype(jnp.int32)
    return (slot_of, packed_of, valid)

def attend(query_row_block, key_row_block, value_row_block, gradient_row_block, key_mask):
    logit_scale = 1.0 / math.sqrt(DH)
    top_precision = lax.Precision.HIGHEST
    logit_scores = jnp.einsum('vlr,vgr->vlg', upcast_single(query_row_block), upcast_single(key_row_block), precision=top_precision) * logit_scale
    logit_scores = jnp.where(key_mask, logit_scores, NEG_FILL)
    exponent = jnp.exp(logit_scores - lax.optimization_barrier(jnp.max(logit_scores, axis=-1, keepdims=True)))
    weights = exponent / lax.optimization_barrier(jnp.sum(exponent, axis=-1, keepdims=True))
    reduced_weights = rounded(weights)
    attention_output = jnp.einsum('hln,hnj->hlj', reduced_weights, upcast_single(value_row_block), precision=top_precision)
    value_gradient = jnp.einsum('fcn,fcz->fnz', reduced_weights, upcast_single(gradient_row_block), precision=top_precision)
    logits_gradient = jnp.einsum('vlr,vgr->vlg', upcast_single(gradient_row_block), upcast_single(value_row_block), precision=top_precision)
    row_delta = lax.optimization_barrier(jnp.sum(weights * logits_gradient, axis=-1, keepdims=True))
    scores_gradient = rounded(weights * (logits_gradient - row_delta) * logit_scale)
    query_gradient = jnp.einsum('hln,hnj->hlj', scores_gradient, upcast_single(key_row_block), precision=top_precision)
    key_gradient = jnp.einsum('fcn,fcz->fnz', scores_gradient, upcast_single(query_row_block), precision=top_precision)
    return (attention_output, query_gradient, key_gradient, value_gradient)

def bands(array):
    return array.reshape(SHARDS, TOK_DEV, HEADS, DH).transpose(0, 2, 1, 3).reshape(SHARDS * HEADS, TOK_DEV, DH)

def unbands(array):
    return array.reshape(SHARDS, HEADS, TOK_DEV, DH).transpose(0, 2, 1, 3).reshape(SEQ, WIDTH)

def band_mask(valid):
    return jnp.repeat(valid.reshape(SHARDS, 1, 1, TOK_DEV), HEADS, axis=1).reshape(SHARDS * HEADS, 1, TOK_DEV)

def reference(queries, key_states, value_states, grad_output, counts, matching):
    zero_low = jnp.zeros((), jnp.bfloat16)

    def one_view(view_index):
        slot_of, packed_of, valid = layout_tables(counts[view_index])
        own_query = queries[view_index]
        own_key = key_states[view_index]
        own_value = value_states[view_index]
        own_grad = jnp.where(valid[:, None], grad_output[view_index], zero_low)

        def heads_first(array):
            return jnp.take(array, slot_of, axis=0).reshape(VIEW_CAP, HEADS, DH).transpose(1, 0, 2)

        def heads_back(array):
            packed = array.transpose(1, 0, 2).reshape(VIEW_CAP, WIDTH).astype(jnp.bfloat16)
            return upcast_single(jnp.take(packed, packed_of, axis=0))
        full_mask = jnp.ones((1, 1, 1), dtype=bool)
        global_parts = attend(heads_first(own_query), heads_first(own_key), heads_first(own_value), heads_first(own_grad), full_mask)
        global_out, global_dq, global_dk, global_dv = [heads_back(part) for part in global_parts]
        right_view = (view_index + 1) % VIEWS
        band_grad = (upcast_single(own_grad) / ROUNDS).astype(jnp.bfloat16)
        zero_wide = jnp.zeros((SEQ, WIDTH), jnp.float32)
        out_sum, dq_sum = (zero_wide, zero_wide)
        left_k, left_v, right_k, right_v = (zero_wide, zero_wide, zero_wide, zero_wide)
        for round_index in range(ROUNDS):
            partner = matching[round_index, view_index]
            partner_valid = layout_tables(counts[partner])[2]
            partner_grad = jnp.where(partner_valid[:, None], grad_output[partner], zero_low)
            partner_grad = (upcast_single(partner_grad) / ROUNDS).astype(jnp.bfloat16)
            out_part, dq_part, unused_k, unused_v = attend(bands(own_query), bands(key_states[partner]), bands(value_states[partner]), bands(band_grad), band_mask(partner_valid))
            unused_o, unused_q, dk_part, dv_part = attend(bands(queries[partner]), bands(own_key), bands(own_value), bands(partner_grad), band_mask(valid))
            out_sum = out_sum + unbands(out_part)
            dq_sum = dq_sum + unbands(dq_part)
            on_right = partner == right_view
            right_k = right_k + jnp.where(on_right, unbands(dk_part), 0.0)
            right_v = right_v + jnp.where(on_right, unbands(dv_part), 0.0)
            left_k = left_k + jnp.where(on_right, 0.0, unbands(dk_part))
            left_v = left_v + jnp.where(on_right, 0.0, unbands(dv_part))
        band_out = rounded(out_sum / ROUNDS)
        keep = valid[:, None]
        attended = jnp.where(keep, (global_out + band_out).astype(jnp.bfloat16), zero_low)
        grad_q = jnp.where(keep, (global_dq + rounded(dq_sum)).astype(jnp.bfloat16), zero_low)
        grad_k = jnp.where(keep, (global_dk + rounded(left_k) + rounded(right_k)).astype(jnp.bfloat16), zero_low)
        grad_v = jnp.where(keep, (global_dv + rounded(left_v) + rounded(right_v)).astype(jnp.bfloat16), zero_low)
        return (attended, grad_q, grad_k, grad_v)
    attended, grad_queries, grad_keys, grad_values = lax.map(one_view, jnp.arange(VIEWS, dtype=jnp.int32))
    return (attended, grad_queries, grad_keys, grad_values)
```

```python
import functools
import math

import jax
import jax.numpy as jnp
from jax import lax
from jax.experimental import pallas as pl
from jax.experimental.pallas import tpu as pltpu
from jax.sharding import PartitionSpec as P

NEG_FILL = -1e30
WIDE = jnp.float32
LOW = jnp.bfloat16


def matmul(left, right, left_dim, right_dim):
    return lax.dot_general(
        left, right, (((left_dim,), (right_dim,)), ((), ())), preferred_element_type=WIDE
    )


def softmax_rows(scores):
    exponent = jnp.exp(scores - jnp.max(scores, axis=-1, keepdims=True))
    return exponent * (1.0 / jnp.sum(exponent, axis=-1, keepdims=True))


def score_gradient(weights, value_gradient, logit_scale):
    row_delta = jnp.sum(weights * value_gradient, axis=-1, keepdims=True)
    return (weights * (value_gradient - row_delta) * logit_scale).astype(LOW)


def split_heads(arrays, group):
    rows, width = arrays[0].shape
    heads = width // 128

    def body(*refs):
        out_ref = refs[-1]
        for j, ref in enumerate(refs[:-1]):
            for h in range(group):
                out_ref[h, j] = ref[:, h * 128 : (h + 1) * 128]

    return pl.pallas_call(
        body,
        grid=(heads // group,),
        in_specs=[pl.BlockSpec((rows, group * 128), lambda i: (0, i))] * len(arrays),
        out_specs=pl.BlockSpec((group, len(arrays), rows, 128), lambda i: (i, 0, 0, 0)),
        out_shape=jax.ShapeDtypeStruct((heads, len(arrays), rows, 128), LOW),
        name="split_heads",
    )(*arrays)


def global_body(counts_ref, x_ref, y_ref, wide_ref, low_ref, back_ref, *, total, logit_scale):
    shards, parts, rows, head_dim = x_ref.shape
    starts = []
    start = 0
    for t in range(shards):
        starts.append(start)
        start = start + counts_ref[t]
    for t in range(shards):
        for j in range(parts):
            wide_ref[j, pl.ds(starts[t], rows), :] = x_ref[t, j].astype(WIDE)
    for j in range(parts):
        low_ref[j] = wide_ref[j, :total].astype(LOW)
    key = low_ref[1]
    value = low_ref[2]
    step = 128
    for at in range(0, total, step):
        query = low_ref[0, at : at + step]
        grad = low_ref[3, at : at + step]
        weights = softmax_rows(matmul(query, key, 1, 1) * logit_scale)
        weights_low = weights.astype(LOW)
        wide_ref[0, at : at + step] = matmul(weights_low, value, 1, 0)
        value_part = matmul(grad, weights_low, 0, 0)
        score_low = score_gradient(weights, matmul(grad, value, 1, 1), logit_scale)
        wide_ref[1, at : at + step] = matmul(score_low, key, 1, 0)
        key_part = matmul(query, score_low, 0, 0)
        if at == 0:
            back_ref[0] = key_part
            back_ref[1] = value_part
        else:
            back_ref[0] += key_part
            back_ref[1] += value_part
    wide_ref[2, :total] = back_ref[0].T
    wide_ref[3, :total] = back_ref[1].T
    for t in range(shards):
        for j in range(parts):
            y_ref[t, j] = wide_ref[j, pl.ds(starts[t], rows), :].astype(LOW)


def global_attention(own_counts, stacked, total, logit_scale):
    shards, parts, rows, head_dim = stacked.shape
    return pl.pallas_call(
        functools.partial(global_body, total=total, logit_scale=logit_scale),
        in_specs=[
            pl.BlockSpec(memory_space=pltpu.SMEM),
            pl.BlockSpec(memory_space=pltpu.VMEM),
        ],
        out_specs=pl.BlockSpec(memory_space=pltpu.VMEM),
        out_shape=jax.ShapeDtypeStruct(stacked.shape, LOW),
        scratch_shapes=[
            pltpu.VMEM((parts, total + rows, head_dim), WIDE),
            pltpu.VMEM((parts, total, head_dim), LOW),
            pltpu.VMEM((2, head_dim, total), WIDE),
        ],
        name="global_attention",
    )(own_counts, stacked)


def band_body(pair_ref, own_ref, other_ref, out_ref, *, logit_scale):
    group, parts, rows, head_dim = own_ref.shape
    own_count = pair_ref[0]
    other_count = pair_ref[1]
    columns = lax.broadcasted_iota(jnp.int32, (rows, rows), 1)
    row_ids = lax.broadcasted_iota(jnp.int32, (rows, head_dim), 0)
    zero_low = jnp.zeros((), LOW)
    for h in range(group):
        query, key, value, grad = (own_ref[h, j] for j in range(4))
        other_query, other_key, other_value, other_grad = (other_ref[h, j] for j in range(4))
        grad = jnp.where(row_ids < own_count, grad, zero_low)
        other_grad = jnp.where(row_ids < other_count, other_grad, zero_low)
        scores = matmul(query, other_key, 1, 1) * logit_scale
        weights = softmax_rows(jnp.where(columns < other_count, scores, NEG_FILL))
        out_ref[h, 0] = matmul(weights.astype(LOW), other_value, 1, 0).astype(LOW)
        score_low = score_gradient(weights, matmul(grad, other_value, 1, 1), logit_scale)
        out_ref[h, 1] = matmul(score_low, other_key, 1, 0).astype(LOW)
        scores = matmul(other_query, key, 1, 1) * logit_scale
        weights = softmax_rows(jnp.where(columns < own_count, scores, NEG_FILL))
        out_ref[h, 3] = matmul(weights.astype(LOW), other_grad, 0, 0).astype(LOW)
        score_low = score_gradient(weights, matmul(other_grad, value, 1, 1), logit_scale)
        out_ref[h, 2] = matmul(score_low, other_query, 0, 0).astype(LOW)


def band_attention(pair_counts, own, other, group, logit_scale):
    heads, parts, rows, head_dim = own.shape
    block = pl.BlockSpec((group, parts, rows, head_dim), lambda i: (i, 0, 0, 0))
    return pl.pallas_call(
        functools.partial(band_body, logit_scale=logit_scale),
        grid=(heads // group,),
        in_specs=[pl.BlockSpec(memory_space=pltpu.SMEM), block, block],
        out_specs=block,
        out_shape=jax.ShapeDtypeStruct(own.shape, LOW),
        name="band_attention",
    )(pair_counts, own, other)


def merge_body(pair_ref, back_ref, band_ref, *out_refs):
    group, parts, rows, head_dim = back_ref.shape
    keep = lax.broadcasted_iota(jnp.int32, (rows, head_dim), 0) < pair_ref[0]
    for j in range(parts):
        for h in range(group):
            total = back_ref[h, j].astype(WIDE) + band_ref[h, j].astype(WIDE)
            out_refs[j][:, h * head_dim : (h + 1) * head_dim] = jnp.where(keep, total, 0.0).astype(
                LOW
            )


def merge(pair_counts, back, band, group):
    heads, parts, rows, head_dim = back.shape
    block = pl.BlockSpec((group, parts, rows, head_dim), lambda i: (i, 0, 0, 0))
    flat = pl.BlockSpec((rows, group * head_dim), lambda i: (0, i))
    return pl.pallas_call(
        merge_body,
        grid=(heads // group,),
        in_specs=[pl.BlockSpec(memory_space=pltpu.SMEM), block, block],
        out_specs=[flat] * parts,
        out_shape=[jax.ShapeDtypeStruct((rows, heads * head_dim), LOW)] * parts,
        name="merge",
    )(pair_counts, back, band)


def exchange(array, on_right, view_index, view_count):
    def swap(parity):
        pairs = [
            (v, (v + 1) % view_count if (v - parity) % 2 == 0 else (v - 1) % view_count)
            for v in range(view_count)
        ]
        return lambda a: lax.ppermute(a, "view", pairs)

    even_first = on_right == (view_index % 2 == 0)
    return lax.cond(even_first, swap(0), swap(1), array)


def to_heads(array):
    return lax.all_to_all(array, "tok", split_axis=0, concat_axis=0, tiled=True)


def view_body(queries, key_states, value_states, grad_output, counts, matching):
    view_index = lax.axis_index("view")
    shard_index = lax.axis_index("tok")
    view_count = lax.axis_size("view")
    shard_count = lax.axis_size("tok")
    shard_rows, row_width = queries.shape
    head_dim = row_width // shard_count
    packed_rows = 5 * shard_rows * shard_count // 16
    logit_scale = 1.0 / math.sqrt(head_dim)
    partner = matching[0, 0]
    on_right = partner == (view_index + 1) % view_count
    own_counts = lax.dynamic_index_in_dim(counts, view_index, 0, keepdims=False)
    pair_counts = jnp.stack([counts[view_index, shard_index], counts[partner, shard_index]])
    stacked = split_heads((queries, key_states, value_states, grad_output), 4)
    gathered = to_heads(stacked)
    other = exchange(stacked, on_right, view_index, view_count)
    band = band_attention(pair_counts, stacked, other, 2, logit_scale)
    back = to_heads(global_attention(own_counts, gathered, packed_rows, logit_scale))
    return merge(pair_counts, back, band, 4)


def per_device(queries, key_states, value_states, grad_output, counts, matching):
    results = view_body(
        queries[0], key_states[0], value_states[0], grad_output[0], counts, matching
    )
    return tuple((result[None] for result in results))


def solution(mesh):
    split = P("view", "tok", None)
    return jax.shard_map(
        per_device,
        mesh=mesh,
        in_specs=(split, split, split, split, P(), P(None, "view")),
        out_specs=(split, split, split, split),
        check_vma=False,
    )
```

```python
import functools
import math

import jax
import jax.numpy as jnp
from jax import lax
from jax.experimental import pallas as pl
from jax.experimental.pallas import tpu as pltpu
from jax.sharding import PartitionSpec as P

NEG_FILL = -1e30
KERNEL_BYTES = 20 << 20
WIDE = jnp.float32
LOW = jnp.bfloat16


def matmul(left, right, left_dim, right_dim):
    return lax.dot_general(
        left, right, (((left_dim,), (right_dim,)), ((), ())), preferred_element_type=WIDE
    )


def softmax_rows(scores):
    exponent = jnp.exp(scores - jnp.max(scores, axis=-1, keepdims=True))
    return exponent * (1.0 / jnp.sum(exponent, axis=-1, keepdims=True))


def score_gradient(weights, value_gradient, logit_scale):
    row_delta = jnp.sum(weights * value_gradient, axis=-1, keepdims=True)
    return (weights * (value_gradient - row_delta) * logit_scale).astype(LOW)


def split_heads(arrays, group):
    rows, width = arrays[0].shape
    heads = width // 128

    def body(*refs):
        out_ref = refs[-1]
        for j, ref in enumerate(refs[:-1]):
            for h in range(group):
                out_ref[h, j] = ref[:, h * 128 : (h + 1) * 128]

    return pl.pallas_call(
        body,
        grid=(heads // group,),
        in_specs=[pl.BlockSpec((rows, group * 128), lambda i: (0, i))] * len(arrays),
        out_specs=pl.BlockSpec((group, len(arrays), rows, 128), lambda i: (i, 0, 0, 0)),
        out_shape=jax.ShapeDtypeStruct((heads, len(arrays), rows, 128), LOW),
        name="split_heads",
    )(*arrays)


def global_body(counts_ref, x_ref, y_ref, wide_ref, low_ref, back_ref, *, total, logit_scale):
    shards, parts, rows, head_dim = x_ref.shape
    starts = []
    start = 0
    for t in range(shards):
        starts.append(start)
        start = start + counts_ref[t]
    for t in range(shards):
        for j in range(parts):
            wide_ref[j, pl.ds(starts[t], rows), :] = x_ref[t, j].astype(WIDE)
    for j in range(parts):
        low_ref[j] = wide_ref[j, :total].astype(LOW)
    key = low_ref[1]
    value = low_ref[2]
    step = 128
    for at in range(0, total, step):
        query = low_ref[0, at : at + step]
        grad = low_ref[3, at : at + step]
        weights = softmax_rows(matmul(query, key, 1, 1) * logit_scale)
        weights_low = weights.astype(LOW)
        wide_ref[0, at : at + step] = matmul(weights_low, value, 1, 0)
        value_part = matmul(grad, weights_low, 0, 0)
        score_low = score_gradient(weights, matmul(grad, value, 1, 1), logit_scale)
        wide_ref[1, at : at + step] = matmul(score_low, key, 1, 0)
        key_part = matmul(query, score_low, 0, 0)
        if at == 0:
            back_ref[0] = key_part
            back_ref[1] = value_part
        else:
            back_ref[0] += key_part
            back_ref[1] += value_part
    wide_ref[2, :total] = back_ref[0].T
    wide_ref[3, :total] = back_ref[1].T
    for t in range(shards):
        for j in range(parts):
            y_ref[t, j] = wide_ref[j, pl.ds(starts[t], rows), :].astype(LOW)


def global_attention(own_counts, stacked, total, logit_scale):
    shards, parts, rows, head_dim = stacked.shape
    return pl.pallas_call(
        functools.partial(global_body, total=total, logit_scale=logit_scale),
        in_specs=[
            pl.BlockSpec(memory_space=pltpu.SMEM),
            pl.BlockSpec(memory_space=pltpu.VMEM),
        ],
        out_specs=pl.BlockSpec(memory_space=pltpu.VMEM),
        out_shape=jax.ShapeDtypeStruct(stacked.shape, LOW),
        scratch_shapes=[
            pltpu.VMEM((parts, total + rows, head_dim), WIDE),
            pltpu.VMEM((parts, total, head_dim), LOW),
            pltpu.VMEM((2, head_dim, total), WIDE),
        ],
        compiler_params=pltpu.CompilerParams(vmem_limit_bytes=KERNEL_BYTES),
        name="global_attention",
    )(own_counts, stacked)


def band_body(pair_ref, own_ref, other_ref, out_ref, *, logit_scale):
    group, parts, rows, head_dim = own_ref.shape
    own_count = pair_ref[0]
    other_count = pair_ref[1]
    columns = lax.broadcasted_iota(jnp.int32, (rows, rows), 1)
    row_ids = lax.broadcasted_iota(jnp.int32, (rows, head_dim), 0)
    zero_low = jnp.zeros((), LOW)
    for h in range(group):
        query, key, value, grad = (own_ref[h, j] for j in range(4))
        other_query, other_key, other_value, other_grad = (other_ref[h, j] for j in range(4))
        grad = jnp.where(row_ids < own_count, grad, zero_low)
        other_grad = jnp.where(row_ids < other_count, other_grad, zero_low)
        scores = matmul(query, other_key, 1, 1) * logit_scale
        weights = softmax_rows(jnp.where(columns < other_count, scores, NEG_FILL))
        out_ref[h, 0] = matmul(weights.astype(LOW), other_value, 1, 0).astype(LOW)
        score_low = score_gradient(weights, matmul(grad, other_value, 1, 1), logit_scale)
        out_ref[h, 1] = matmul(score_low, other_key, 1, 0).astype(LOW)
        scores = matmul(other_query, key, 1, 1) * logit_scale
        weights = softmax_rows(jnp.where(columns < own_count, scores, NEG_FILL))
        out_ref[h, 3] = matmul(weights.astype(LOW), other_grad, 0, 0).astype(LOW)
        score_low = score_gradient(weights, matmul(other_grad, value, 1, 1), logit_scale)
        out_ref[h, 2] = matmul(score_low, other_query, 0, 0).astype(LOW)


def band_attention(pair_counts, own, other, group, logit_scale):
    heads, parts, rows, head_dim = own.shape
    block = pl.BlockSpec((group, parts, rows, head_dim), lambda i: (i, 0, 0, 0))
    return pl.pallas_call(
        functools.partial(band_body, logit_scale=logit_scale),
        grid=(heads // group,),
        in_specs=[pl.BlockSpec(memory_space=pltpu.SMEM), block, block],
        out_specs=block,
        out_shape=jax.ShapeDtypeStruct(own.shape, LOW),
        compiler_params=pltpu.CompilerParams(vmem_limit_bytes=KERNEL_BYTES),
        name="band_attention",
    )(pair_counts, own, other)


def merge_body(pair_ref, back_ref, band_ref, *out_refs):
    group, parts, rows, head_dim = back_ref.shape
    keep = lax.broadcasted_iota(jnp.int32, (rows, head_dim), 0) < pair_ref[0]
    for j in range(parts):
        for h in range(group):
            total = back_ref[h, j].astype(WIDE) + band_ref[h, j].astype(WIDE)
            out_refs[j][:, h * head_dim : (h + 1) * head_dim] = jnp.where(keep, total, 0.0).astype(
                LOW
            )


def merge(pair_counts, back, band, group):
    heads, parts, rows, head_dim = back.shape
    block = pl.BlockSpec((group, parts, rows, head_dim), lambda i: (i, 0, 0, 0))
    flat = pl.BlockSpec((rows, group * head_dim), lambda i: (0, i))
    return pl.pallas_call(
        merge_body,
        grid=(heads // group,),
        in_specs=[pl.BlockSpec(memory_space=pltpu.SMEM), block, block],
        out_specs=[flat] * parts,
        out_shape=[jax.ShapeDtypeStruct((rows, heads * head_dim), LOW)] * parts,
        compiler_params=pltpu.CompilerParams(vmem_limit_bytes=KERNEL_BYTES),
        name="merge",
    )(pair_counts, back, band)


def exchange(array, on_right, view_index, view_count):
    def swap(parity):
        pairs = [
            (v, (v + 1) % view_count if (v - parity) % 2 == 0 else (v - 1) % view_count)
            for v in range(view_count)
        ]
        return lambda a: lax.ppermute(a, "view", pairs)

    even_first = on_right == (view_index % 2 == 0)
    return lax.cond(even_first, swap(0), swap(1), array)


def to_heads(array):
    return lax.all_to_all(array, "tok", split_axis=0, concat_axis=0, tiled=True)


def view_body(queries, key_states, value_states, grad_output, counts, matching):
    view_index = lax.axis_index("view")
    shard_index = lax.axis_index("tok")
    view_count = lax.axis_size("view")
    shard_count = lax.axis_size("tok")
    shard_rows, row_width = queries.shape
    head_dim = row_width // shard_count
    packed_rows = 5 * shard_rows * shard_count // 16
    logit_scale = 1.0 / math.sqrt(head_dim)
    partner = matching[0, 0]
    on_right = partner == (view_index + 1) % view_count
    own_counts = lax.dynamic_index_in_dim(counts, view_index, 0, keepdims=False)
    pair_counts = jnp.stack([counts[view_index, shard_index], counts[partner, shard_index]])
    stacked = split_heads((queries, key_states, value_states, grad_output), 4)
    gathered = to_heads(stacked)
    other = exchange(stacked, on_right, view_index, view_count)
    band = band_attention(pair_counts, stacked, other, 2, logit_scale)
    gathered, band = lax.optimization_barrier((gathered, band))
    back = to_heads(global_attention(own_counts, gathered, packed_rows, logit_scale))
    return merge(pair_counts, back, band, 4)


def per_device(queries, key_states, value_states, grad_output, counts, matching):
    results = view_body(
        queries[0], key_states[0], value_states[0], grad_output[0], counts, matching
    )
    return tuple((result[None] for result in results))


def solution(mesh):
    split = P("view", "tok", None)
    return jax.shard_map(
        per_device,
        mesh=mesh,
        in_specs=(split, split, split, split, P(), P(None, "view")),
        out_specs=(split, split, split, split),
        check_vma=False,
    )
```

```python
import functools
import math

import jax
import jax.numpy as jnp
from jax import lax
from jax.experimental import pallas as pl
from jax.experimental.pallas import tpu as pltpu
from jax.sharding import PartitionSpec as P

NEG_FILL = -1e30
KERNEL_BYTES = 20 << 20
BAND_HEADS = 4
WIDE = jnp.float32
LOW = jnp.bfloat16


def matmul(left, right, left_dim, right_dim):
    return lax.dot_general(
        left, right, (((left_dim,), (right_dim,)), ((), ())), preferred_element_type=WIDE
    )


def softmax_rows(scores):
    exponent = jnp.exp(scores - jnp.max(scores, axis=-1, keepdims=True))
    return exponent * (1.0 / jnp.sum(exponent, axis=-1, keepdims=True))


def score_gradient(weights, value_gradient, logit_scale):
    row_delta = jnp.sum(weights * value_gradient, axis=-1, keepdims=True)
    return (weights * (value_gradient - row_delta) * logit_scale).astype(LOW)


def split_heads(arrays, group):
    rows, width = arrays[0].shape
    heads = width // 128

    def body(*refs):
        out_ref = refs[-1]
        for j, ref in enumerate(refs[:-1]):
            for h in range(group):
                out_ref[h, j] = ref[:, h * 128 : (h + 1) * 128]

    return pl.pallas_call(
        body,
        grid=(heads // group,),
        in_specs=[pl.BlockSpec((rows, group * 128), lambda i: (0, i))] * len(arrays),
        out_specs=pl.BlockSpec((group, len(arrays), rows, 128), lambda i: (i, 0, 0, 0)),
        out_shape=jax.ShapeDtypeStruct((heads, len(arrays), rows, 128), LOW),
        name="split_heads",
    )(*arrays)


def global_body(counts_ref, x_ref, y_ref, wide_ref, low_ref, back_ref, *, total, logit_scale):
    shards, parts, rows, head_dim = x_ref.shape
    starts = []
    start = 0
    for t in range(shards):
        starts.append(start)
        start = start + counts_ref[t]
    for t in range(shards):
        for j in range(parts):
            wide_ref[j, pl.ds(starts[t], rows), :] = x_ref[t, j].astype(WIDE)
    for j in range(parts):
        low_ref[j] = wide_ref[j, :total].astype(LOW)
    key = low_ref[1]
    value = low_ref[2]
    step = 128
    for at in range(0, total, step):
        query = low_ref[0, at : at + step]
        grad = low_ref[3, at : at + step]
        weights = softmax_rows(matmul(query, key, 1, 1) * logit_scale)
        weights_low = weights.astype(LOW)
        wide_ref[0, at : at + step] = matmul(weights_low, value, 1, 0)
        value_part = matmul(grad, weights_low, 0, 0)
        score_low = score_gradient(weights, matmul(grad, value, 1, 1), logit_scale)
        wide_ref[1, at : at + step] = matmul(score_low, key, 1, 0)
        key_part = matmul(query, score_low, 0, 0)
        if at == 0:
            back_ref[0] = key_part
            back_ref[1] = value_part
        else:
            back_ref[0] += key_part
            back_ref[1] += value_part
    wide_ref[2, :total] = back_ref[0].T
    wide_ref[3, :total] = back_ref[1].T
    for t in range(shards):
        for j in range(parts):
            y_ref[t, j] = wide_ref[j, pl.ds(starts[t], rows), :].astype(LOW)


def global_attention(own_counts, stacked, total, logit_scale):
    shards, parts, rows, head_dim = stacked.shape
    return pl.pallas_call(
        functools.partial(global_body, total=total, logit_scale=logit_scale),
        in_specs=[
            pl.BlockSpec(memory_space=pltpu.SMEM),
            pl.BlockSpec(memory_space=pltpu.VMEM),
        ],
        out_specs=pl.BlockSpec(memory_space=pltpu.VMEM),
        out_shape=jax.ShapeDtypeStruct(stacked.shape, LOW),
        scratch_shapes=[
            pltpu.VMEM((parts, total + rows, head_dim), WIDE),
            pltpu.VMEM((parts, total, head_dim), LOW),
            pltpu.VMEM((2, head_dim, total), WIDE),
        ],
        compiler_params=pltpu.CompilerParams(vmem_limit_bytes=KERNEL_BYTES),
        name="global_attention",
    )(own_counts, stacked)


def band_body(pair_ref, own_ref, other_ref, out_ref, *, logit_scale):
    group, parts, rows, head_dim = own_ref.shape
    own_count = pair_ref[0]
    other_count = pair_ref[1]
    columns = lax.broadcasted_iota(jnp.int32, (rows, rows), 1)
    row_ids = lax.broadcasted_iota(jnp.int32, (rows, head_dim), 0)
    zero_low = jnp.zeros((), LOW)
    own = [[own_ref[h, j] for j in range(4)] for h in range(group)]
    other = [[other_ref[h, j] for j in range(4)] for h in range(group)]
    for h in range(group):
        own[h][3] = jnp.where(row_ids < own_count, own[h][3], zero_low)
        other[h][3] = jnp.where(row_ids < other_count, other[h][3], zero_low)
    sides = [(own[h], other[h], other_count) for h in range(group)]
    sides += [(other[h], own[h], own_count) for h in range(group)]
    scores = [matmul(a[0], b[1], 1, 1) for a, b, count in sides]
    gradients = [matmul(a[3], b[2], 1, 1) for a, b, count in sides]
    weights = [
        softmax_rows(jnp.where(columns < side[2], part * logit_scale, NEG_FILL))
        for part, side in zip(scores, sides)
    ]
    weights_low = [part.astype(LOW) for part in weights]
    score_low = [
        score_gradient(part, gradient, logit_scale) for part, gradient in zip(weights, gradients)
    ]
    for h in range(group):
        out_ref[h, 0] = matmul(weights_low[h], other[h][2], 1, 0).astype(LOW)
        out_ref[h, 1] = matmul(score_low[h], other[h][1], 1, 0).astype(LOW)
        out_ref[h, 2] = matmul(score_low[group + h], other[h][0], 0, 0).astype(LOW)
        out_ref[h, 3] = matmul(weights_low[group + h], other[h][3], 0, 0).astype(LOW)


def band_attention(pair_counts, own, other, group, logit_scale):
    heads, parts, rows, head_dim = own.shape
    block = pl.BlockSpec((group, parts, rows, head_dim), lambda i: (i, 0, 0, 0))
    return pl.pallas_call(
        functools.partial(band_body, logit_scale=logit_scale),
        grid=(heads // group,),
        in_specs=[pl.BlockSpec(memory_space=pltpu.SMEM), block, block],
        out_specs=block,
        out_shape=jax.ShapeDtypeStruct(own.shape, LOW),
        compiler_params=pltpu.CompilerParams(vmem_limit_bytes=KERNEL_BYTES),
        name="band_attention",
    )(pair_counts, own, other)


def merge_body(pair_ref, back_ref, band_ref, *out_refs):
    group, parts, rows, head_dim = back_ref.shape
    keep = lax.broadcasted_iota(jnp.int32, (rows, head_dim), 0) < pair_ref[0]
    for j in range(parts):
        for h in range(group):
            total = back_ref[h, j].astype(WIDE) + band_ref[h, j].astype(WIDE)
            out_refs[j][:, h * head_dim : (h + 1) * head_dim] = jnp.where(keep, total, 0.0).astype(
                LOW
            )


def merge(pair_counts, back, band, group):
    heads, parts, rows, head_dim = back.shape
    block = pl.BlockSpec((group, parts, rows, head_dim), lambda i: (i, 0, 0, 0))
    flat = pl.BlockSpec((rows, group * head_dim), lambda i: (0, i))
    return pl.pallas_call(
        merge_body,
        grid=(heads // group,),
        in_specs=[pl.BlockSpec(memory_space=pltpu.SMEM), block, block],
        out_specs=[flat] * parts,
        out_shape=[jax.ShapeDtypeStruct((rows, heads * head_dim), LOW)] * parts,
        compiler_params=pltpu.CompilerParams(vmem_limit_bytes=KERNEL_BYTES),
        name="merge",
    )(pair_counts, back, band)


def exchange(array, on_right, view_index, view_count):
    def swap(parity):
        pairs = [
            (v, (v + 1) % view_count if (v - parity) % 2 == 0 else (v - 1) % view_count)
            for v in range(view_count)
        ]
        return lambda a: lax.ppermute(a, "view", pairs)

    even_first = on_right == (view_index % 2 == 0)
    return lax.cond(even_first, swap(0), swap(1), array)


def to_heads(array):
    return lax.all_to_all(array, "tok", split_axis=0, concat_axis=0, tiled=True)


def view_body(queries, key_states, value_states, grad_output, counts, matching):
    view_index = lax.axis_index("view")
    shard_index = lax.axis_index("tok")
    view_count = lax.axis_size("view")
    shard_count = lax.axis_size("tok")
    shard_rows, row_width = queries.shape
    head_dim = row_width // shard_count
    packed_rows = 5 * shard_rows * shard_count // 16
    logit_scale = 1.0 / math.sqrt(head_dim)
    partner = matching[0, 0]
    on_right = partner == (view_index + 1) % view_count
    own_counts = lax.dynamic_index_in_dim(counts, view_index, 0, keepdims=False)
    pair_counts = jnp.stack([counts[view_index, shard_index], counts[partner, shard_index]])
    stacked = split_heads((queries, key_states, value_states, grad_output), 4)
    gathered = to_heads(stacked)
    other = exchange(stacked, on_right, view_index, view_count)
    band = band_attention(pair_counts, stacked, other, BAND_HEADS, logit_scale)
    gathered, band = lax.optimization_barrier((gathered, band))
    parts = global_attention(own_counts, gathered, packed_rows, logit_scale)
    back = to_heads(parts)
    return merge(pair_counts, back, band, 4)


def per_device(queries, key_states, value_states, grad_output, counts, matching):
    results = view_body(
        queries[0], key_states[0], value_states[0], grad_output[0], counts, matching
    )
    return tuple((result[None] for result in results))


def solution(mesh):
    split = P("view", "tok", None)
    return jax.shard_map(
        per_device,
        mesh=mesh,
        in_specs=(split, split, split, split, P(), P(None, "view")),
        out_specs=(split, split, split, split),
        check_vma=False,
    )
```

```python
import functools
import math

import jax
import jax.numpy as jnp
from jax import lax
from jax.experimental import pallas as pl
from jax.experimental.pallas import tpu as pltpu
from jax.sharding import PartitionSpec as P

NEG_FILL = -1e30
KERNEL_BYTES = 20 << 20
BAND_HEADS = 4
HOLD_NS = 12000
WIDE = jnp.float32
LOW = jnp.bfloat16


def matmul(left, right, left_dim, right_dim):
    return lax.dot_general(
        left, right, (((left_dim,), (right_dim,)), ((), ())), preferred_element_type=WIDE
    )


def softmax_rows(scores):
    exponent = jnp.exp(scores - jnp.max(scores, axis=-1, keepdims=True))
    return exponent * (1.0 / jnp.sum(exponent, axis=-1, keepdims=True))


def score_gradient(weights, value_gradient, logit_scale):
    row_delta = jnp.sum(weights * value_gradient, axis=-1, keepdims=True)
    return (weights * (value_gradient - row_delta) * logit_scale).astype(LOW)


def split_heads(held, arrays, group):
    rows, width = arrays[0].shape
    heads = width // 128

    def body(held_ref, *refs):
        @pl.when((pl.program_id(0) == 0) & (held_ref[0] == 1))
        def _():
            pl.delay(HOLD_NS)

        out_ref = refs[-1]
        for j, ref in enumerate(refs[:-1]):
            for h in range(group):
                out_ref[h, j] = ref[:, h * 128 : (h + 1) * 128]

    return pl.pallas_call(
        body,
        grid=(heads // group,),
        in_specs=[pl.BlockSpec(memory_space=pltpu.SMEM)]
        + [pl.BlockSpec((rows, group * 128), lambda i: (0, i))] * len(arrays),
        out_specs=pl.BlockSpec((group, len(arrays), rows, 128), lambda i: (i, 0, 0, 0)),
        out_shape=jax.ShapeDtypeStruct((heads, len(arrays), rows, 128), LOW),
        name="split_heads",
    )(held, *arrays)


def global_body(counts_ref, x_ref, y_ref, wide_ref, low_ref, back_ref, *, total, logit_scale):
    shards, parts, rows, head_dim = x_ref.shape
    starts = []
    start = 0
    for t in range(shards):
        starts.append(start)
        start = start + counts_ref[t]
    for t in range(shards):
        for j in range(parts):
            wide_ref[j, pl.ds(starts[t], rows), :] = x_ref[t, j].astype(WIDE)
    for j in range(parts):
        low_ref[j] = wide_ref[j, :total].astype(LOW)
    key = low_ref[1]
    value = low_ref[2]
    step = 128
    spans = [slice(at, at + step) for at in range(0, total, step)]
    queries = [low_ref[0, span] for span in spans]
    grads = [low_ref[3, span] for span in spans]
    scores = [matmul(query, key, 1, 1) for query in queries]
    gradients = [matmul(grad, value, 1, 1) for grad in grads]
    weights = [softmax_rows(part * logit_scale) for part in scores]
    weights_low = [part.astype(LOW) for part in weights]
    for span, part in zip(spans, weights_low):
        wide_ref[0, span] = matmul(part, value, 1, 0)
    back_ref[1] = sum(matmul(grad, part, 0, 0) for grad, part in zip(grads, weights_low))
    score_low = [
        score_gradient(part, gradient, logit_scale) for part, gradient in zip(weights, gradients)
    ]
    for span, part in zip(spans, score_low):
        wide_ref[1, span] = matmul(part, key, 1, 0)
    back_ref[0] = sum(matmul(query, part, 0, 0) for query, part in zip(queries, score_low))
    wide_ref[2, :total] = back_ref[0].T
    wide_ref[3, :total] = back_ref[1].T
    for t in range(shards):
        for j in range(parts):
            y_ref[t, j] = wide_ref[j, pl.ds(starts[t], rows), :].astype(LOW)


def global_attention(own_counts, stacked, total, logit_scale):
    shards, parts, rows, head_dim = stacked.shape
    return pl.pallas_call(
        functools.partial(global_body, total=total, logit_scale=logit_scale),
        in_specs=[
            pl.BlockSpec(memory_space=pltpu.SMEM),
            pl.BlockSpec(memory_space=pltpu.VMEM),
        ],
        out_specs=pl.BlockSpec(memory_space=pltpu.VMEM),
        out_shape=jax.ShapeDtypeStruct(stacked.shape, LOW),
        scratch_shapes=[
            pltpu.VMEM((parts, total + rows, head_dim), WIDE),
            pltpu.VMEM((parts, total, head_dim), LOW),
            pltpu.VMEM((2, head_dim, total), WIDE),
        ],
        compiler_params=pltpu.CompilerParams(vmem_limit_bytes=KERNEL_BYTES),
        name="global_attention",
    )(own_counts, stacked)


def band_body(pair_ref, own_ref, other_ref, out_ref, *, logit_scale):
    group, parts, rows, head_dim = own_ref.shape
    own_count = pair_ref[0]
    other_count = pair_ref[1]
    columns = lax.broadcasted_iota(jnp.int32, (rows, rows), 1)
    row_ids = lax.broadcasted_iota(jnp.int32, (rows, head_dim), 0)
    zero_low = jnp.zeros((), LOW)
    own = [[own_ref[h, j] for j in range(4)] for h in range(group)]
    other = [[other_ref[h, j] for j in range(4)] for h in range(group)]
    for h in range(group):
        own[h][3] = jnp.where(row_ids < own_count, own[h][3], zero_low)
        other[h][3] = jnp.where(row_ids < other_count, other[h][3], zero_low)
    sides = [(own[h], other[h], other_count) for h in range(group)]
    sides += [(other[h], own[h], own_count) for h in range(group)]
    scores = [matmul(a[0], b[1], 1, 1) for a, b, count in sides]
    gradients = [matmul(a[3], b[2], 1, 1) for a, b, count in sides]
    weights = [
        softmax_rows(jnp.where(columns < side[2], part * logit_scale, NEG_FILL))
        for part, side in zip(scores, sides)
    ]
    weights_low = [part.astype(LOW) for part in weights]
    score_low = [
        score_gradient(part, gradient, logit_scale) for part, gradient in zip(weights, gradients)
    ]
    for h in range(group):
        out_ref[h, 0] = matmul(weights_low[h], other[h][2], 1, 0).astype(LOW)
        out_ref[h, 1] = matmul(score_low[h], other[h][1], 1, 0).astype(LOW)
        out_ref[h, 2] = matmul(score_low[group + h], other[h][0], 0, 0).astype(LOW)
        out_ref[h, 3] = matmul(weights_low[group + h], other[h][3], 0, 0).astype(LOW)


def band_attention(pair_counts, own, other, group, logit_scale):
    heads, parts, rows, head_dim = own.shape
    block = pl.BlockSpec((group, parts, rows, head_dim), lambda i: (i, 0, 0, 0))
    return pl.pallas_call(
        functools.partial(band_body, logit_scale=logit_scale),
        grid=(heads // group,),
        in_specs=[pl.BlockSpec(memory_space=pltpu.SMEM), block, block],
        out_specs=block,
        out_shape=jax.ShapeDtypeStruct(own.shape, LOW),
        compiler_params=pltpu.CompilerParams(vmem_limit_bytes=KERNEL_BYTES),
        name="band_attention",
    )(pair_counts, own, other)


def merge_body(pair_ref, back_ref, band_ref, *out_refs):
    group, parts, rows, head_dim = back_ref.shape
    keep = lax.broadcasted_iota(jnp.int32, (rows, head_dim), 0) < pair_ref[0]
    for j in range(parts):
        for h in range(group):
            total = back_ref[h, j].astype(WIDE) + band_ref[h, j].astype(WIDE)
            out_refs[j][:, h * head_dim : (h + 1) * head_dim] = jnp.where(keep, total, 0.0).astype(
                LOW
            )


def merge(pair_counts, back, band, group):
    heads, parts, rows, head_dim = back.shape
    block = pl.BlockSpec((group, parts, rows, head_dim), lambda i: (i, 0, 0, 0))
    flat = pl.BlockSpec((rows, group * head_dim), lambda i: (0, i))
    return pl.pallas_call(
        merge_body,
        grid=(heads // group,),
        in_specs=[pl.BlockSpec(memory_space=pltpu.SMEM), block, block],
        out_specs=[flat] * parts,
        out_shape=[jax.ShapeDtypeStruct((rows, heads * head_dim), LOW)] * parts,
        compiler_params=pltpu.CompilerParams(vmem_limit_bytes=KERNEL_BYTES),
        name="merge",
    )(pair_counts, back, band)


def exchange(array, on_right, view_index, view_count):
    def swap(parity):
        pairs = [
            (v, (v + 1) % view_count if (v - parity) % 2 == 0 else (v - 1) % view_count)
            for v in range(view_count)
        ]
        return lambda a: lax.ppermute(a, "view", pairs)

    even_first = on_right == (view_index % 2 == 0)
    return lax.cond(even_first, swap(0), swap(1), array)


def to_heads(array):
    return lax.all_to_all(array, "tok", split_axis=0, concat_axis=0, tiled=True)


def view_body(queries, key_states, value_states, grad_output, counts, matching):
    view_index = lax.axis_index("view")
    shard_index = lax.axis_index("tok")
    view_count = lax.axis_size("view")
    shard_count = lax.axis_size("tok")
    shard_rows, row_width = queries.shape
    head_dim = row_width // shard_count
    packed_rows = 5 * shard_rows * shard_count // 16
    logit_scale = 1.0 / math.sqrt(head_dim)
    partner = matching[0, 0]
    on_right = partner == (view_index + 1) % view_count
    own_counts = lax.dynamic_index_in_dim(counts, view_index, 0, keepdims=False)
    pair_counts = jnp.stack([counts[view_index, shard_index], counts[partner, shard_index]])
    held = (3 * view_index < view_count).astype(jnp.int32).reshape(1)
    stacked = split_heads(held, (queries, key_states, value_states, grad_output), 4)
    gathered = to_heads(stacked)
    other = exchange(stacked, on_right, view_index, view_count)
    band = band_attention(pair_counts, stacked, other, BAND_HEADS, logit_scale)
    gathered, band = lax.optimization_barrier((gathered, band))
    parts = global_attention(own_counts, gathered, packed_rows, logit_scale)
    back = to_heads(parts)
    return merge(pair_counts, back, band, 4)


def per_device(queries, key_states, value_states, grad_output, counts, matching):
    results = view_body(
        queries[0], key_states[0], value_states[0], grad_output[0], counts, matching
    )
    return tuple((result[None] for result in results))


def solution(mesh):
    split = P("view", "tok", None)
    return jax.shard_map(
        per_device,
        mesh=mesh,
        in_specs=(split, split, split, split, P(), P(None, "view")),
        out_specs=(split, split, split, split),
        check_vma=False,
    )
```

```python
import functools
import math

import jax
import jax.numpy as jnp
from jax import lax
from jax.experimental import pallas as pl
from jax.experimental.pallas import tpu as pltpu
from jax.sharding import PartitionSpec as P

NEG_FILL = -1e30
KERNEL_BYTES = 20 << 20
BAND_HEADS = 4
HOLD_NS = 6000
WIDE = jnp.float32
LOW = jnp.bfloat16


def matmul(left, right, left_dim, right_dim):
    return lax.dot_general(
        left, right, (((left_dim,), (right_dim,)), ((), ())), preferred_element_type=WIDE
    )


def softmax_rows(scores):
    exponent = jnp.exp(scores - jnp.max(scores, axis=-1, keepdims=True))
    return exponent * (1.0 / jnp.sum(exponent, axis=-1, keepdims=True))


def score_gradient(weights, value_gradient, logit_scale):
    row_delta = jnp.sum(weights * value_gradient, axis=-1, keepdims=True)
    return (weights * (value_gradient - row_delta) * logit_scale).astype(LOW)


def split_heads(held, arrays, group):
    rows, width = arrays[0].shape
    heads = width // 128

    def body(held_ref, *refs):
        @pl.when((pl.program_id(0) == 0) & (held_ref[0] == 1))
        def _():
            pl.delay(HOLD_NS)

        out_ref = refs[-1]
        for j, ref in enumerate(refs[:-1]):
            for h in range(group):
                out_ref[h, j] = ref[:, h * 128 : (h + 1) * 128]

    return pl.pallas_call(
        body,
        grid=(heads // group,),
        in_specs=[pl.BlockSpec(memory_space=pltpu.SMEM)]
        + [pl.BlockSpec((rows, group * 128), lambda i: (0, i))] * len(arrays),
        out_specs=pl.BlockSpec((group, len(arrays), rows, 128), lambda i: (i, 0, 0, 0)),
        out_shape=jax.ShapeDtypeStruct((heads, len(arrays), rows, 128), LOW),
        name="split_heads",
    )(held, *arrays)


def global_body(counts_ref, x_ref, y_ref, wide_ref, low_ref, back_ref, *, total, logit_scale):
    shards, parts, rows, head_dim = x_ref.shape
    starts = []
    start = 0
    for t in range(shards):
        starts.append(start)
        start = start + counts_ref[t]
    for t in range(shards):
        for j in range(parts):
            wide_ref[j, pl.ds(starts[t], rows), :] = x_ref[t, j].astype(WIDE)
    for j in range(parts):
        low_ref[j] = wide_ref[j, :total].astype(LOW)
    key = low_ref[1]
    value = low_ref[2]
    step = 128
    spans = [slice(at, at + step) for at in range(0, total, step)]
    queries = [low_ref[0, span] for span in spans]
    grads = [low_ref[3, span] for span in spans]
    scores = [matmul(query, key, 1, 1) for query in queries]
    gradients = [matmul(grad, value, 1, 1) for grad in grads]
    weights = [softmax_rows(part * logit_scale) for part in scores]
    weights_low = [part.astype(LOW) for part in weights]
    for span, part in zip(spans, weights_low):
        wide_ref[0, span] = matmul(part, value, 1, 0)
    back_ref[1] = sum(matmul(grad, part, 0, 0) for grad, part in zip(grads, weights_low))
    score_low = [
        score_gradient(part, gradient, logit_scale) for part, gradient in zip(weights, gradients)
    ]
    for span, part in zip(spans, score_low):
        wide_ref[1, span] = matmul(part, key, 1, 0)
    back_ref[0] = sum(matmul(query, part, 0, 0) for query, part in zip(queries, score_low))
    wide_ref[2, :total] = back_ref[0].T
    wide_ref[3, :total] = back_ref[1].T
    for t in range(shards):
        for j in range(parts):
            y_ref[t, j] = wide_ref[j, pl.ds(starts[t], rows), :].astype(LOW)


def global_attention(own_counts, stacked, total, logit_scale):
    shards, parts, rows, head_dim = stacked.shape
    return pl.pallas_call(
        functools.partial(global_body, total=total, logit_scale=logit_scale),
        in_specs=[
            pl.BlockSpec(memory_space=pltpu.SMEM),
            pl.BlockSpec(memory_space=pltpu.VMEM),
        ],
        out_specs=pl.BlockSpec(memory_space=pltpu.VMEM),
        out_shape=jax.ShapeDtypeStruct(stacked.shape, LOW),
        scratch_shapes=[
            pltpu.VMEM((parts, total + rows, head_dim), WIDE),
            pltpu.VMEM((parts, total, head_dim), LOW),
            pltpu.VMEM((2, head_dim, total), WIDE),
        ],
        compiler_params=pltpu.CompilerParams(vmem_limit_bytes=KERNEL_BYTES),
        name="global_attention",
    )(own_counts, stacked)


def band_body(pair_ref, own_ref, other_ref, out_ref, *, logit_scale):
    group, parts, rows, head_dim = own_ref.shape
    own_count = pair_ref[0]
    other_count = pair_ref[1]
    columns = lax.broadcasted_iota(jnp.int32, (rows, rows), 1)
    row_ids = lax.broadcasted_iota(jnp.int32, (rows, head_dim), 0)
    zero_low = jnp.zeros((), LOW)
    own = [[own_ref[h, j] for j in range(4)] for h in range(group)]
    other = [[other_ref[h, j] for j in range(4)] for h in range(group)]
    for h in range(group):
        own[h][3] = jnp.where(row_ids < own_count, own[h][3], zero_low)
        other[h][3] = jnp.where(row_ids < other_count, other[h][3], zero_low)
    sides = [(own[h], other[h], other_count) for h in range(group)]
    sides += [(other[h], own[h], own_count) for h in range(group)]
    scores = [matmul(a[0], b[1], 1, 1) for a, b, count in sides]
    gradients = [matmul(a[3], b[2], 1, 1) for a, b, count in sides]
    weights = [
        softmax_rows(jnp.where(columns < side[2], part * logit_scale, NEG_FILL))
        for part, side in zip(scores, sides)
    ]
    weights_low = [part.astype(LOW) for part in weights]
    score_low = [
        score_gradient(part, gradient, logit_scale) for part, gradient in zip(weights, gradients)
    ]
    for h in range(group):
        out_ref[h, 0] = matmul(weights_low[h], other[h][2], 1, 0).astype(LOW)
        out_ref[h, 1] = matmul(score_low[h], other[h][1], 1, 0).astype(LOW)
        out_ref[h, 2] = matmul(score_low[group + h], other[h][0], 0, 0).astype(LOW)
        out_ref[h, 3] = matmul(weights_low[group + h], other[h][3], 0, 0).astype(LOW)


def band_attention(pair_counts, own, other, group, logit_scale):
    heads, parts, rows, head_dim = own.shape
    block = pl.BlockSpec((group, parts, rows, head_dim), lambda i: (i, 0, 0, 0))
    return pl.pallas_call(
        functools.partial(band_body, logit_scale=logit_scale),
        grid=(heads // group,),
        in_specs=[pl.BlockSpec(memory_space=pltpu.SMEM), block, block],
        out_specs=block,
        out_shape=jax.ShapeDtypeStruct(own.shape, LOW),
        compiler_params=pltpu.CompilerParams(vmem_limit_bytes=KERNEL_BYTES),
        name="band_attention",
    )(pair_counts, own, other)


def merge_body(pair_ref, back_ref, band_ref, *out_refs):
    group, parts, rows, head_dim = back_ref.shape
    keep = lax.broadcasted_iota(jnp.int32, (rows, head_dim), 0) < pair_ref[0]
    for j in range(parts):
        for h in range(group):
            total = back_ref[h, j].astype(WIDE) + band_ref[h, j].astype(WIDE)
            out_refs[j][:, h * head_dim : (h + 1) * head_dim] = jnp.where(keep, total, 0.0).astype(
                LOW
            )


def merge(pair_counts, back, band, group):
    heads, parts, rows, head_dim = back.shape
    block = pl.BlockSpec((group, parts, rows, head_dim), lambda i: (i, 0, 0, 0))
    flat = pl.BlockSpec((rows, group * head_dim), lambda i: (0, i))
    return pl.pallas_call(
        merge_body,
        grid=(heads // group,),
        in_specs=[pl.BlockSpec(memory_space=pltpu.SMEM), block, block],
        out_specs=[flat] * parts,
        out_shape=[jax.ShapeDtypeStruct((rows, heads * head_dim), LOW)] * parts,
        compiler_params=pltpu.CompilerParams(vmem_limit_bytes=KERNEL_BYTES),
        name="merge",
    )(pair_counts, back, band)


def exchange(array, on_right, view_index, view_count):
    def swap(parity):
        pairs = [
            (v, (v + 1) % view_count if (v - parity) % 2 == 0 else (v - 1) % view_count)
            for v in range(view_count)
        ]
        return lambda a: lax.ppermute(a, "view", pairs)

    even_first = on_right == (view_index % 2 == 0)
    return lax.cond(even_first, swap(0), swap(1), array)


def to_heads(array):
    return lax.all_to_all(array, "tok", split_axis=0, concat_axis=0, tiled=True)


def view_body(queries, key_states, value_states, grad_output, counts, matching):
    view_index = lax.axis_index("view")
    shard_index = lax.axis_index("tok")
    view_count = lax.axis_size("view")
    shard_count = lax.axis_size("tok")
    shard_rows, row_width = queries.shape
    head_dim = row_width // shard_count
    packed_rows = 5 * shard_rows * shard_count // 16
    logit_scale = 1.0 / math.sqrt(head_dim)
    partner = matching[0, 0]
    on_right = partner == (view_index + 1) % view_count
    own_counts = lax.dynamic_index_in_dim(counts, view_index, 0, keepdims=False)
    pair_counts = jnp.stack([counts[view_index, shard_index], counts[partner, shard_index]])
    held = (3 * view_index < view_count).astype(jnp.int32).reshape(1)
    stacked = split_heads(held, (queries, key_states, value_states, grad_output), 4)
    gathered = to_heads(stacked)
    other = exchange(stacked, on_right, view_index, view_count)
    band = band_attention(pair_counts, stacked, other, BAND_HEADS, logit_scale)
    gathered, band = lax.optimization_barrier((gathered, band))
    parts = global_attention(own_counts, gathered, packed_rows, logit_scale)
    back = to_heads(parts)
    return merge(pair_counts, back, band, 4)


def per_device(queries, key_states, value_states, grad_output, counts, matching):
    results = view_body(
        queries[0], key_states[0], value_states[0], grad_output[0], counts, matching
    )
    return tuple((result[None] for result in results))


def solution(mesh):
    split = P("view", "tok", None)
    return jax.shard_map(
        per_device,
        mesh=mesh,
        in_specs=(split, split, split, split, P(), P(None, "view")),
        out_specs=(split, split, split, split),
        check_vma=False,
    )
```

```python
import functools
import math

import jax
import jax.numpy as jnp
from jax import lax
from jax.experimental import pallas as pl
from jax.experimental.pallas import tpu as pltpu
from jax.sharding import PartitionSpec as P

NEG_FILL = -1e30
KERNEL_BYTES = 20 << 20
BAND_HEADS = 4
HOLD_NS = 6000
WIDE = jnp.float32
LOW = jnp.bfloat16


def matmul(left, right, left_dim, right_dim):
    return lax.dot_general(
        left, right, (((left_dim,), (right_dim,)), ((), ())), preferred_element_type=WIDE
    )


def softmax_rows(scores):
    exponent = jnp.exp(scores - jnp.max(scores, axis=-1, keepdims=True))
    return exponent * (1.0 / jnp.sum(exponent, axis=-1, keepdims=True))


def score_gradient(weights, value_gradient, logit_scale):
    row_delta = jnp.sum(weights * value_gradient, axis=-1, keepdims=True)
    return (weights * (value_gradient - row_delta) * logit_scale).astype(LOW)


def split_heads(view, matching, view_count, arrays, group):
    rows, width = arrays[0].shape
    heads = width // 128

    def body(view_ref, matching_ref, *refs):
        own = view_ref[0]
        right = jnp.where(own + 1 == view_count, 0, own + 1)
        partner = jnp.where(own % 2 == 0, right, own - 1)
        early = (matching_ref[0, 0] == partner) & (3 * own < view_count)

        @pl.when((pl.program_id(0) == 0) & early)
        def _():
            pl.delay(HOLD_NS)

        out_ref = refs[-1]
        for j, ref in enumerate(refs[:-1]):
            for h in range(group):
                out_ref[h, j] = ref[:, h * 128 : (h + 1) * 128]

    return pl.pallas_call(
        body,
        grid=(heads // group,),
        in_specs=[pl.BlockSpec(memory_space=pltpu.SMEM)] * 2
        + [pl.BlockSpec((rows, group * 128), lambda i: (0, i))] * len(arrays),
        out_specs=pl.BlockSpec((group, len(arrays), rows, 128), lambda i: (i, 0, 0, 0)),
        out_shape=jax.ShapeDtypeStruct((heads, len(arrays), rows, 128), LOW),
        name="split_heads",
    )(view, matching, *arrays)


def global_body(counts_ref, x_ref, y_ref, wide_ref, low_ref, back_ref, *, total, logit_scale):
    shards, parts, rows, head_dim = x_ref.shape
    starts = []
    start = 0
    for t in range(shards):
        starts.append(start)
        start = start + counts_ref[t]
    for t in range(shards):
        for j in range(parts):
            wide_ref[j, pl.ds(starts[t], rows), :] = x_ref[t, j].astype(WIDE)
    for j in range(parts):
        low_ref[j] = wide_ref[j, :total].astype(LOW)
    key = low_ref[1]
    value = low_ref[2]
    step = 128
    spans = [slice(at, at + step) for at in range(0, total, step)]
    queries = [low_ref[0, span] for span in spans]
    grads = [low_ref[3, span] for span in spans]
    scores = [matmul(query, key, 1, 1) for query in queries]
    gradients = [matmul(grad, value, 1, 1) for grad in grads]
    weights = [softmax_rows(part * logit_scale) for part in scores]
    weights_low = [part.astype(LOW) for part in weights]
    for span, part in zip(spans, weights_low):
        wide_ref[0, span] = matmul(part, value, 1, 0)
    back_ref[1] = sum(matmul(grad, part, 0, 0) for grad, part in zip(grads, weights_low))
    score_low = [
        score_gradient(part, gradient, logit_scale) for part, gradient in zip(weights, gradients)
    ]
    for span, part in zip(spans, score_low):
        wide_ref[1, span] = matmul(part, key, 1, 0)
    back_ref[0] = sum(matmul(query, part, 0, 0) for query, part in zip(queries, score_low))
    wide_ref[2, :total] = back_ref[0].T
    wide_ref[3, :total] = back_ref[1].T
    for t in range(shards):
        for j in range(parts):
            y_ref[t, j] = wide_ref[j, pl.ds(starts[t], rows), :].astype(LOW)


def global_attention(own_counts, stacked, total, logit_scale):
    shards, parts, rows, head_dim = stacked.shape
    return pl.pallas_call(
        functools.partial(global_body, total=total, logit_scale=logit_scale),
        in_specs=[
            pl.BlockSpec(memory_space=pltpu.SMEM),
            pl.BlockSpec(memory_space=pltpu.VMEM),
        ],
        out_specs=pl.BlockSpec(memory_space=pltpu.VMEM),
        out_shape=jax.ShapeDtypeStruct(stacked.shape, LOW),
        scratch_shapes=[
            pltpu.VMEM((parts, total + rows, head_dim), WIDE),
            pltpu.VMEM((parts, total, head_dim), LOW),
            pltpu.VMEM((2, head_dim, total), WIDE),
        ],
        compiler_params=pltpu.CompilerParams(vmem_limit_bytes=KERNEL_BYTES),
        name="global_attention",
    )(own_counts, stacked)


def band_body(pair_ref, own_ref, other_ref, out_ref, *, logit_scale):
    group, parts, rows, head_dim = own_ref.shape
    own_count = pair_ref[0]
    other_count = pair_ref[1]
    columns = lax.broadcasted_iota(jnp.int32, (rows, rows), 1)
    row_ids = lax.broadcasted_iota(jnp.int32, (rows, head_dim), 0)
    zero_low = jnp.zeros((), LOW)
    own = [[own_ref[h, j] for j in range(4)] for h in range(group)]
    other = [[other_ref[h, j] for j in range(4)] for h in range(group)]
    for h in range(group):
        own[h][3] = jnp.where(row_ids < own_count, own[h][3], zero_low)
        other[h][3] = jnp.where(row_ids < other_count, other[h][3], zero_low)
    sides = [(own[h], other[h], other_count) for h in range(group)]
    sides += [(other[h], own[h], own_count) for h in range(group)]
    scores = [matmul(a[0], b[1], 1, 1) for a, b, count in sides]
    gradients = [matmul(a[3], b[2], 1, 1) for a, b, count in sides]
    weights = [
        softmax_rows(jnp.where(columns < side[2], part * logit_scale, NEG_FILL))
        for part, side in zip(scores, sides)
    ]
    weights_low = [part.astype(LOW) for part in weights]
    score_low = [
        score_gradient(part, gradient, logit_scale) for part, gradient in zip(weights, gradients)
    ]
    for h in range(group):
        out_ref[h, 0] = matmul(weights_low[h], other[h][2], 1, 0).astype(LOW)
        out_ref[h, 1] = matmul(score_low[h], other[h][1], 1, 0).astype(LOW)
        out_ref[h, 2] = matmul(score_low[group + h], other[h][0], 0, 0).astype(LOW)
        out_ref[h, 3] = matmul(weights_low[group + h], other[h][3], 0, 0).astype(LOW)


def band_attention(pair_counts, own, other, group, logit_scale):
    heads, parts, rows, head_dim = own.shape
    block = pl.BlockSpec((group, parts, rows, head_dim), lambda i: (i, 0, 0, 0))
    return pl.pallas_call(
        functools.partial(band_body, logit_scale=logit_scale),
        grid=(heads // group,),
        in_specs=[pl.BlockSpec(memory_space=pltpu.SMEM), block, block],
        out_specs=block,
        out_shape=jax.ShapeDtypeStruct(own.shape, LOW),
        compiler_params=pltpu.CompilerParams(vmem_limit_bytes=KERNEL_BYTES),
        name="band_attention",
    )(pair_counts, own, other)


def merge_body(pair_ref, back_ref, band_ref, *out_refs):
    group, parts, rows, head_dim = back_ref.shape
    keep = lax.broadcasted_iota(jnp.int32, (rows, head_dim), 0) < pair_ref[0]
    for j in range(parts):
        for h in range(group):
            total = back_ref[h, j].astype(WIDE) + band_ref[h, j].astype(WIDE)
            out_refs[j][:, h * head_dim : (h + 1) * head_dim] = jnp.where(keep, total, 0.0).astype(
                LOW
            )


def merge(pair_counts, back, band, group):
    heads, parts, rows, head_dim = back.shape
    block = pl.BlockSpec((group, parts, rows, head_dim), lambda i: (i, 0, 0, 0))
    flat = pl.BlockSpec((rows, group * head_dim), lambda i: (0, i))
    return pl.pallas_call(
        merge_body,
        grid=(heads // group,),
        in_specs=[pl.BlockSpec(memory_space=pltpu.SMEM), block, block],
        out_specs=[flat] * parts,
        out_shape=[jax.ShapeDtypeStruct((rows, heads * head_dim), LOW)] * parts,
        compiler_params=pltpu.CompilerParams(vmem_limit_bytes=KERNEL_BYTES),
        name="merge",
    )(pair_counts, back, band)


def exchange(array, on_right, view_index, view_count):
    def swap(parity):
        pairs = [
            (v, (v + 1) % view_count if (v - parity) % 2 == 0 else (v - 1) % view_count)
            for v in range(view_count)
        ]
        return lambda a: lax.ppermute(a, "view", pairs)

    even_first = on_right == (view_index % 2 == 0)
    return lax.cond(even_first, swap(0), swap(1), array)


def to_heads(array):
    return lax.all_to_all(array, "tok", split_axis=0, concat_axis=0, tiled=True)


def view_body(queries, key_states, value_states, grad_output, counts, matching):
    view_index = lax.axis_index("view")
    shard_index = lax.axis_index("tok")
    view_count = lax.axis_size("view")
    shard_count = lax.axis_size("tok")
    shard_rows, row_width = queries.shape
    head_dim = row_width // shard_count
    packed_rows = 5 * shard_rows * shard_count // 16
    logit_scale = 1.0 / math.sqrt(head_dim)
    partner = matching[0, 0]
    on_right = partner == (view_index + 1) % view_count
    own_counts = lax.dynamic_index_in_dim(counts, view_index, 0, keepdims=False)
    pair_counts = jnp.stack([counts[view_index, shard_index], counts[partner, shard_index]])
    stacked = split_heads(
        view_index.reshape(1),
        matching,
        view_count,
        (queries, key_states, value_states, grad_output),
        4,
    )
    gathered = to_heads(stacked)
    other = exchange(stacked, on_right, view_index, view_count)
    band = band_attention(pair_counts, stacked, other, BAND_HEADS, logit_scale)
    gathered, band = lax.optimization_barrier((gathered, band))
    parts = global_attention(own_counts, gathered, packed_rows, logit_scale)
    back = to_heads(parts)
    return merge(pair_counts, back, band, 4)


def per_device(queries, key_states, value_states, grad_output, counts, matching):
    results = view_body(
        queries[0], key_states[0], value_states[0], grad_output[0], counts, matching
    )
    return tuple((result[None] for result in results))


def solution(mesh):
    split = P("view", "tok", None)
    return jax.shard_map(
        per_device,
        mesh=mesh,
        in_specs=(split, split, split, split, P(), P(None, "view")),
        out_specs=(split, split, split, split),
        check_vma=False,
    )
```

```python
import functools
import math

import jax
import jax.numpy as jnp
from jax import lax
from jax.experimental import pallas as pl
from jax.experimental.pallas import tpu as pltpu
from jax.sharding import PartitionSpec as P

NEG_FILL = -1e30
KERNEL_BYTES = 20 << 20
BAND_HEADS = 4
HOLD_NS = 6000
WIDE = jnp.float32
LOW = jnp.bfloat16


def matmul(left, right, left_dim, right_dim):
    return lax.dot_general(
        left, right, (((left_dim,), (right_dim,)), ((), ())), preferred_element_type=WIDE
    )


def softmax_rows(scores):
    exponent = jnp.exp(scores - jnp.max(scores, axis=-1, keepdims=True))
    return exponent * (1.0 / jnp.sum(exponent, axis=-1, keepdims=True))


def score_gradient(weights, value_gradient, logit_scale):
    row_delta = jnp.sum(weights * value_gradient, axis=-1, keepdims=True)
    return (weights * (value_gradient - row_delta) * logit_scale).astype(LOW)


def split_heads(view, matching, view_count, arrays, group):
    rows, width = arrays[0].shape
    heads = width // 128

    def body(view_ref, matching_ref, *refs):
        own = view_ref[0]
        right = jnp.where(own + 1 == view_count, 0, own + 1)
        partner = jnp.where(own % 2 == 0, right, own - 1)
        early = (matching_ref[0, 0] == partner) & (3 * own < view_count)

        @pl.when((pl.program_id(0) == 0) & early)
        def _():
            pl.delay(HOLD_NS)

        out_ref = refs[-1]
        for j, ref in enumerate(refs[:-1]):
            for h in range(group):
                out_ref[h, j] = ref[:, h * 128 : (h + 1) * 128]

    return pl.pallas_call(
        body,
        grid=(heads // group,),
        in_specs=[pl.BlockSpec(memory_space=pltpu.SMEM)] * 2
        + [pl.BlockSpec((rows, group * 128), lambda i: (0, i))] * len(arrays),
        out_specs=pl.BlockSpec((group, len(arrays), rows, 128), lambda i: (i, 0, 0, 0)),
        out_shape=jax.ShapeDtypeStruct((heads, len(arrays), rows, 128), LOW),
        name="split_heads",
    )(view, matching, *arrays)


def global_body(counts_ref, x_ref, y_ref, wide_ref, low_ref, back_ref, *, total, logit_scale):
    shards, parts, rows, head_dim = x_ref.shape
    starts = []
    start = 0
    for t in range(shards):
        starts.append(start)
        start = start + counts_ref[t]
    for t in range(shards):
        for j in range(parts):
            wide_ref[j, pl.ds(starts[t], rows), :] = x_ref[t, j].astype(WIDE)
    for j in range(parts):
        low_ref[j] = wide_ref[j, :total].astype(LOW)
    key = low_ref[1]
    value = low_ref[2]
    step = 128
    spans = [slice(at, at + step) for at in range(0, total, step)]
    queries = [low_ref[0, span] for span in spans]
    grads = [low_ref[3, span] for span in spans]
    scores = [matmul(query, key, 1, 1) for query in queries]
    gradients = [matmul(grad, value, 1, 1) for grad in grads]
    weights = [softmax_rows(part * logit_scale) for part in scores]
    weights_low = [part.astype(LOW) for part in weights]
    for span, part in zip(spans, weights_low):
        wide_ref[0, span] = matmul(part, value, 1, 0)
    back_ref[1] = sum(matmul(grad, part, 0, 0) for grad, part in zip(grads, weights_low))
    score_low = [
        score_gradient(part, gradient, logit_scale) for part, gradient in zip(weights, gradients)
    ]
    for span, part in zip(spans, score_low):
        wide_ref[1, span] = matmul(part, key, 1, 0)
    back_ref[0] = sum(matmul(query, part, 0, 0) for query, part in zip(queries, score_low))
    wide_ref[2, :total] = back_ref[0].T
    wide_ref[3, :total] = back_ref[1].T
    for t in range(shards):
        for j in range(parts):
            y_ref[t, j] = wide_ref[j, pl.ds(starts[t], rows), :].astype(LOW)


def global_attention(own_counts, stacked, total, logit_scale):
    shards, parts, rows, head_dim = stacked.shape
    return pl.pallas_call(
        functools.partial(global_body, total=total, logit_scale=logit_scale),
        in_specs=[
            pl.BlockSpec(memory_space=pltpu.SMEM),
            pl.BlockSpec(memory_space=pltpu.VMEM),
        ],
        out_specs=pl.BlockSpec(memory_space=pltpu.VMEM),
        out_shape=jax.ShapeDtypeStruct(stacked.shape, LOW),
        scratch_shapes=[
            pltpu.VMEM((parts, total + rows, head_dim), WIDE),
            pltpu.VMEM((parts, total, head_dim), LOW),
            pltpu.VMEM((2, head_dim, total), WIDE),
        ],
        compiler_params=pltpu.CompilerParams(vmem_limit_bytes=KERNEL_BYTES),
        name="global_attention",
    )(own_counts, stacked)


def band_body(pair_ref, own_ref, other_ref, out_ref, *, logit_scale):
    group, parts, rows, head_dim = own_ref.shape
    own_count = pair_ref[0]
    other_count = pair_ref[1]
    columns = lax.broadcasted_iota(jnp.int32, (rows, rows), 1)
    row_ids = lax.broadcasted_iota(jnp.int32, (rows, head_dim), 0)
    zero_low = jnp.zeros((), LOW)
    own = [[own_ref[h, j] for j in range(4)] for h in range(group)]
    other = [[other_ref[h, j] for j in range(4)] for h in range(group)]
    for h in range(group):
        own[h][3] = jnp.where(row_ids < own_count, own[h][3], zero_low)
        other[h][3] = jnp.where(row_ids < other_count, other[h][3], zero_low)
    sides = [(own[h], other[h], other_count) for h in range(group)]
    sides += [(other[h], own[h], own_count) for h in range(group)]
    scores = [matmul(a[0], b[1], 1, 1) for a, b, count in sides]
    gradients = [matmul(a[3], b[2], 1, 1) for a, b, count in sides]
    weights = [
        softmax_rows(jnp.where(columns < side[2], part * logit_scale, NEG_FILL))
        for part, side in zip(scores, sides)
    ]
    weights_low = [part.astype(LOW) for part in weights]
    score_low = [
        score_gradient(part, gradient, logit_scale) for part, gradient in zip(weights, gradients)
    ]
    for h in range(group):
        out_ref[h, 0] = matmul(weights_low[h], other[h][2], 1, 0).astype(LOW)
        out_ref[h, 1] = matmul(score_low[h], other[h][1], 1, 0).astype(LOW)
        out_ref[h, 2] = matmul(score_low[group + h], other[h][0], 0, 0).astype(LOW)
        out_ref[h, 3] = matmul(weights_low[group + h], other[h][3], 0, 0).astype(LOW)


def band_attention(pair_counts, own, other, group, logit_scale):
    heads, parts, rows, head_dim = own.shape
    block = pl.BlockSpec((group, parts, rows, head_dim), lambda i: (i, 0, 0, 0))
    return pl.pallas_call(
        functools.partial(band_body, logit_scale=logit_scale),
        grid=(heads // group,),
        in_specs=[pl.BlockSpec(memory_space=pltpu.SMEM), block, block],
        out_specs=block,
        out_shape=jax.ShapeDtypeStruct(own.shape, LOW),
        compiler_params=pltpu.CompilerParams(vmem_limit_bytes=KERNEL_BYTES),
        name="band_attention",
    )(pair_counts, own, other)


def merge_body(pair_ref, back_ref, band_ref, *out_refs):
    group, parts, rows, head_dim = back_ref.shape
    keep = lax.broadcasted_iota(jnp.int32, (rows, head_dim), 0) < pair_ref[0]
    for j in range(parts):
        for h in range(group):
            total = back_ref[h, j].astype(WIDE) + band_ref[h, j].astype(WIDE)
            out_refs[j][:, h * head_dim : (h + 1) * head_dim] = jnp.where(keep, total, 0.0).astype(
                LOW
            )


def merge(pair_counts, back, band, group):
    heads, parts, rows, head_dim = back.shape
    block = pl.BlockSpec((group, parts, rows, head_dim), lambda i: (i, 0, 0, 0))
    flat = pl.BlockSpec((rows, group * head_dim), lambda i: (0, i))
    return pl.pallas_call(
        merge_body,
        grid=(heads // group,),
        in_specs=[pl.BlockSpec(memory_space=pltpu.SMEM), block, block],
        out_specs=[flat] * parts,
        out_shape=[jax.ShapeDtypeStruct((rows, heads * head_dim), LOW)] * parts,
        compiler_params=pltpu.CompilerParams(vmem_limit_bytes=KERNEL_BYTES),
        name="merge",
    )(pair_counts, back, band)


def exchange(array, even_first, pairs_of):
    def swap(parity):
        pairs = pairs_of(parity)
        if not pairs:
            return jnp.zeros_like
        return lambda a: lax.ppermute(a, "view", pairs)

    return lax.cond(even_first, swap(0), swap(1), array)


def to_heads(array):
    return lax.all_to_all(array, "tok", split_axis=0, concat_axis=0, tiled=True)


def view_body(queries, key_states, value_states, grad_output, counts, matching):
    view_index = lax.axis_index("view")
    shard_index = lax.axis_index("tok")
    view_count = lax.axis_size("view")
    shard_count = lax.axis_size("tok")
    shard_rows, row_width = queries.shape
    head_dim = row_width // shard_count
    packed_rows = 5 * shard_rows * shard_count // 16
    logit_scale = 1.0 / math.sqrt(head_dim)
    partner = matching[0, 0]
    on_right = partner == (view_index + 1) % view_count
    own_counts = lax.dynamic_index_in_dim(counts, view_index, 0, keepdims=False)
    pair_counts = jnp.stack([counts[view_index, shard_index], counts[partner, shard_index]])
    stacked = split_heads(
        view_index.reshape(1),
        matching,
        view_count,
        (queries, key_states, value_states, grad_output),
        4,
    )
    third = view_count // 3
    even_first = on_right == (view_index % 2 == 0)

    def pairs_of(parity, far):
        pairs = []
        for v in range(view_count):
            w = (v + 1 if (v - parity) % 2 == 0 else v - 1) % view_count
            if (v // third != w // third) == far:
                pairs.append((v, w))
        return pairs

    far_other = exchange(stacked, even_first, functools.partial(pairs_of, far=True))
    stacked, far_other = lax.optimization_barrier((stacked, far_other))
    gathered = to_heads(stacked)
    near_other = exchange(stacked, even_first, functools.partial(pairs_of, far=False))
    other = jnp.where(view_index // third == partner // third, near_other, far_other)
    band = band_attention(pair_counts, stacked, other, BAND_HEADS, logit_scale)
    gathered, band = lax.optimization_barrier((gathered, band))
    parts = global_attention(own_counts, gathered, packed_rows, logit_scale)
    back = to_heads(parts)
    return merge(pair_counts, back, band, 4)


def per_device(queries, key_states, value_states, grad_output, counts, matching):
    results = view_body(
        queries[0], key_states[0], value_states[0], grad_output[0], counts, matching
    )
    return tuple((result[None] for result in results))


def solution(mesh):
    split = P("view", "tok", None)
    return jax.shard_map(
        per_device,
        mesh=mesh,
        in_specs=(split, split, split, split, P(), P(None, "view")),
        out_specs=(split, split, split, split),
        check_vma=False,
    )
```
